1024 devices in a mesh: expert: 64 (over z, x_hi, core), tensor: 8 (over y), dp: 2 (over x_lo).
Axes of the slice: x: 4 (x_hi: 2, x_lo: 2; x = x_hi * 2 + x_lo), y: 8, z: 16, core: 2. Of those that a mesh axis runs over, the one named last changes fastest.
Arguments:
- attn_out: bfloat16 [8192, 8192], P('expert', ('tensor', 'dp')), may hold values from -6 to 6
- out_weight: bfloat16 [8192, 3584], P(('tensor', 'dp')), may hold values from -0.0625 to 0.0625
- residual: bfloat16 [8192, 3584], P(('expert', 'dp'), 'tensor'), may hold values from -38 to 38
- norm_gain: float32 [3584], replicated, may hold values from 0.25 to 1.75
- gate_weights: bfloat16 [64, 3584, 2048], P('expert', None, 'tensor'), may hold values from -0.09375 to 0.09375
- up_weights: bfloat16 [64, 3584, 2048], P('expert', None, 'tensor'), may hold values from -0.09375 to 0.09375
- down_weights: bfloat16 [64, 2048, 3584], P('expert', 'tensor'), may hold values from -0.125 to 0.125
- routes: int32 [8192, 8], P(('expert', 'dp')), may hold values from 0 to 63, as said below
- gate_values: int32 [8192, 8], P(('expert', 'dp')), may hold values from 1 to 16
Outputs:
- mixed: bfloat16 [8192, 3584], P(('expert', 'dp'), 'tensor')
The draws below stay inside these ranges and needn't reach their ends.
Inputs may be any that keep to these rules, and one draw needn't show every extreme that they name: `routes`: each row names 8 different experts. In each aligned block of 64 rows (the rows of one device), every expert is named by exactly 8 rows.
All inputs are finite; a program needn't handle non-finite values.
Results may differ from the reference program's by a relative error of at most 0.015.
Values may be sent and summed in bfloat16 or wider, within the bound.
No kernel may reach another device: no remote copies, remote signals or barrier semaphores. Data moves between devices by JAX's collectives and lax.ppermute only.
A program may use at most 64 MiB of HBM per device.

```python
import math
import jax
import jax.numpy as jnp
from jax import lax

D = 3584
FF = 2048
EXPERTS = 64
TOPK = 8
TOK_DEV = 64
CAPACITY = 8
TOKENS = 8192
HV = 8192
N_TENSOR = 8


def draw_routes(key, part):
    blocks_total = TOKENS // TOK_DEV
    class_count = EXPERTS // TOPK
    block_keys = jax.random.split(jax.random.fold_in(key, 11), blocks_total)

    def per_block(subkey):
        first_key, second_key = jax.random.split(subkey)
        ranking = jax.random.permutation(first_key, EXPERTS).astype(jnp.int32)
        seating = jax.random.permutation(second_key, TOK_DEV).astype(jnp.int32)
        classes = seating % class_count
        chosen_at = classes[:, None] + class_count * jnp.arange(TOPK, dtype=jnp.int32)[None, :]
        return ranking[chosen_at]
    return jax.vmap(per_block)(block_keys).reshape(TOKENS, TOPK).astype(jnp.int32)


def draw_residual(key, part):
    first_key, second_key, third_key = jax.random.split(jax.random.fold_in(key, 23), 3)
    row_scale = jnp.exp(jax.random.uniform(first_key, (TOKENS, 1), jnp.float32, math.log(0.4), math.log(2.5)))
    column_scale = jnp.exp(jax.random.uniform(second_key, (1, D), jnp.float32, math.log(0.4), math.log(2.5)))
    values = jnp.clip(jax.random.normal(third_key, (TOKENS, D), jnp.float32), -6.0, 6.0)
    return (values * row_scale * column_scale).astype(jnp.bfloat16)


def plant(values, own_key, smallest, high):
    shape = values.shape
    index_at = [jax.random.randint(jax.random.fold_in(own_key, axis), (), 0, shape[axis]) for axis in range(len(shape))]
    values = values.at[tuple(index_at)].set(smallest)
    longest = shape.index(max(shape))
    index_at[longest] = (index_at[longest] + 1) % shape[longest]
    return values.at[tuple(index_at)].set(high)


def level_of(rng, extent, shards, smallest, largest):
    loudness, own = 1.0, jax.random.fold_in(rng, 6)
    for dim, shards_of in shards:
        steps = jnp.exp(jax.random.uniform(jax.random.fold_in(own, dim), (shards_of,), jnp.float32, smallest / len(shards), largest / len(shards)))
        loudness = loudness * jnp.repeat(steps, extent[dim] // shards_of).reshape([-1 if axis == dim else 1 for axis in range(len(extent))])
    return loudness


def noise(key, extent, spread, bound, cuts=(), kind=jnp.bfloat16):
    drawn = jax.random.normal(key, extent, jnp.float32) * spread
    if len(cuts) > 0:
        drawn = level_of(key, extent, cuts, -0.22, 0.18) * drawn
    return jnp.clip(drawn, min=-bound, max=bound).astype(kind)


def setup_inputs(seed: int = 0) -> dict:
    key_of = jax.random.split(jax.random.key(seed), 10)
    attn_out = noise(key_of[0], (TOKENS, HV), 1.0, 6.0, ((0, 64), (1, 16)))
    out_weight = noise(key_of[1], (HV, D), HV ** -0.5, 0.0625, ((0, 16),))
    residual = draw_residual(jax.random.fold_in(key_of[9], 71), 0)
    norm_gain = jnp.clip(1.0 + 0.15 * jax.random.normal(key_of[3], (D,), jnp.float32), 0.25, 1.75)
    gate_weights = noise(key_of[4], (EXPERTS, D, FF), D ** -0.5, 0.09375, ((0, 64), (2, 8)))
    up_weights = noise(key_of[5], (EXPERTS, D, FF), D ** -0.5, 0.09375, ((0, 64), (2, 8)))
    down_weights = noise(key_of[6], (EXPERTS, FF, D), FF ** -0.5, 0.125, ((0, 64), (1, 8)))
    routes = draw_routes(jax.random.fold_in(key_of[9], 71), 0)
    gate_values = plant(jax.random.randint(key_of[8], (TOKENS, TOPK), 1, 17), jax.random.fold_in(key_of[8], 1), 1, 16).astype(jnp.int32)
    return {"attn_out": attn_out, "out_weight": out_weight, "residual": residual, "norm_gain": norm_gain, "gate_weights": gate_weights, "up_weights": up_weights, "down_weights": down_weights, "routes": routes, "gate_values": gate_values}


norm_eps = 1e-06
route_scale = 2.5

def reference(attn_out, out_weight, residual, norm_gain, gate_weights, up_weights, down_weights, routes, gate_values):
    attn = jnp.dot(attn_out, out_weight, preferred_element_type=jnp.float32)
    stream = (residual.astype(jnp.float32) + attn).astype(jnp.bfloat16)
    stream_wide = stream.astype(jnp.float32)
    inverse = lax.rsqrt(lax.optimization_barrier(jnp.mean(stream_wide * stream_wide, axis=1)) + norm_eps)
    scaled = (stream_wide * norm_gain.astype(jnp.float32)).astype(jnp.bfloat16)
    gate_float = gate_values.astype(jnp.float32)
    mix_weight = (route_scale * gate_float / lax.optimization_barrier(jnp.sum(gate_float, axis=1, keepdims=True))).astype(jnp.bfloat16)
    blocks_total = TOKENS // TOK_DEV
    per_block = routes.reshape(blocks_total, TOK_DEV * TOPK)
    onehot = (per_block[:, :, None] == jnp.arange(EXPERTS, dtype=jnp.int32)[None, None, :]).astype(jnp.int32)
    earlier = jnp.cumsum(onehot, axis=1) - onehot
    slot = lax.optimization_barrier(jnp.sum(onehot * earlier, axis=2)).astype(jnp.int32)
    position = (jnp.arange(blocks_total, dtype=jnp.int32)[:, None] * CAPACITY + slot).reshape(-1).astype(jnp.int32)
    flat_expert = routes.reshape(-1).astype(jnp.int32)
    token_of = jnp.repeat(jnp.arange(TOKENS, dtype=jnp.int32), TOPK)
    table = jnp.full((EXPERTS, blocks_total * CAPACITY), TOKENS, jnp.int32).at[flat_expert, position].set(token_of)
    scaled_pad = jnp.concatenate([scaled, jnp.zeros((1, D), jnp.bfloat16)], axis=0)
    inverse_pad = jnp.concatenate([inverse, jnp.zeros((1,), jnp.float32)], axis=0)
    part_width = FF // N_TENSOR

    def run_expert(expert):
        rows_in = scaled_pad[table[expert]]
        factor = inverse_pad[table[expert]][:, None]
        gate = factor * jnp.dot(rows_in, gate_weights[expert], preferred_element_type=jnp.float32)
        up = factor * jnp.dot(rows_in, up_weights[expert], preferred_element_type=jnp.float32)
        hidden = (jax.nn.silu(gate) * up).astype(jnp.bfloat16)
        pieces = jnp.einsum('snf,nfd->nsd', hidden.reshape(-1, N_TENSOR, part_width).astype(jnp.float32), down_weights[expert].reshape(N_TENSOR, part_width, D).astype(jnp.float32))
        rounded = lax.optimization_barrier(pieces.astype(jnp.bfloat16))
        return lax.optimization_barrier(jnp.sum(rounded.astype(jnp.float32), axis=0)).astype(jnp.bfloat16)
    outputs = lax.map(run_expert, jnp.arange(EXPERTS, dtype=jnp.int32))
    picked = outputs[flat_expert, position].astype(jnp.float32).reshape(TOKENS, TOPK, D)
    moe = lax.optimization_barrier(jnp.sum(picked * mix_weight.astype(jnp.float32)[:, :, None], axis=1))
    return (stream_wide + moe).astype(jnp.bfloat16)
```

```python
import functools

import jax
import jax.numpy as jnp
from jax import lax
from jax.experimental import pallas as pl
from jax.experimental.pallas import tpu as pltpu
from jax.sharding import PartitionSpec as P

norm_eps = 1e-06
route_scale = 2.5
bf16 = jnp.bfloat16
f32 = jnp.float32


def mm(a, b, contract=(1, 0)):
    return lax.dot_general(
        a, b, (((contract[0],), (contract[1],)), ((), ())), preferred_element_type=f32
    )


def project_kernel(attn_ref, weight_ref, out_ref):
    own_half = out_ref.shape[2]
    part = out_ref.shape[3] // 2
    value = mm(attn_ref[...], weight_ref[...]).astype(bf16)
    for j in range(2):
        for d in range(out_ref.shape[1]):
            for h in range(2):
                row = (d * 2 + h) * own_half
                out_ref[j, d, :, h * part : (h + 1) * part] = value[
                    row : row + own_half, j * part : (j + 1) * part
                ]


def project(attn_out, out_weight, tensor_count, dp_count):
    rows, depth = attn_out.shape
    width = out_weight.shape[1]
    part = width // tensor_count
    own = rows // dp_count
    return pl.pallas_call(
        project_kernel,
        grid=(tensor_count // 2,),
        in_specs=[
            pl.BlockSpec((rows, depth), lambda s: (0, 0)),
            pl.BlockSpec((depth, 2 * part), lambda s: (0, s)),
        ],
        out_specs=pl.BlockSpec((2, dp_count, own // 2, 2 * part), lambda s: (s, 0, 0, 0)),
        out_shape=jax.ShapeDtypeStruct((tensor_count, dp_count, own // 2, 2 * part), bf16),
        name="project",
    )(attn_out, out_weight)


def slots_of(routes, experts, half):
    own = routes.shape[1]
    expert_row = lax.broadcasted_iota(jnp.int32, (experts, own), 0)
    named = jnp.zeros((experts, own), f32)
    for k in range(routes.shape[0]):
        named = named + jnp.where(routes[k : k + 1, :] == expert_row, 1.0, 0.0)
    before = jnp.where(
        lax.broadcasted_iota(jnp.int32, (own, own), 0)
        < lax.broadcasted_iota(jnp.int32, (own, own), 1),
        1.0,
        0.0,
    ).astype(bf16)
    slot = mm(named.astype(bf16), before)
    row = lax.broadcasted_iota(jnp.int32, (experts * half, experts), 0)
    col = lax.broadcasted_iota(jnp.int32, (experts * half, experts), 1)
    repeat = jnp.where(row // half == col, 1.0, 0.0).astype(bf16)
    slot_rows = mm(repeat, slot.astype(bf16))
    place = (lax.broadcasted_iota(jnp.int32, (experts * half, own), 0) % half).astype(f32)
    return named, repeat, slot_rows, place, expert_row


def dispatch_kernel(experts, parts_ref, residual_ref, routes_ref, stream_ref, sent_ref):
    rows, wide = sent_ref.shape
    part = wide // 2
    half = rows // experts
    total = parts_ref[0].astype(f32)
    for i in range(1, parts_ref.shape[0]):
        total = total + parts_ref[i].astype(f32)
    attn = jnp.concatenate([total[:, :part], total[:, part:]], axis=0)
    stream = (residual_ref[...].astype(f32) + attn).astype(bf16)
    stream_ref[...] = stream
    named, repeat, slot_rows, place, _ = slots_of(routes_ref[...], experts, half)
    named_rows = mm(repeat, named.astype(bf16))
    for h in range(2):
        pick = jnp.where(slot_rows == place + h * half, named_rows, 0.0).astype(bf16)
        sent_ref[:, h * part : (h + 1) * part] = mm(pick, stream).astype(bf16)


def expert_kernel(steps, x_ref, gain_ref, gate_ref, up_ref, down_ref, out_ref, gate_acc, up_acc, square_acc, hidden):
    step = pl.program_id(0)
    part = gate_ref.shape[0]
    rows = x_ref.shape[1]
    width = part * steps

    @pl.when(step == 0)
    def _():
        gate_acc[...] = jnp.zeros_like(gate_acc)
        up_acc[...] = jnp.zeros_like(up_acc)
        square_acc[...] = jnp.zeros_like(square_acc)

    @pl.when(step < steps)
    def _():
        for h in range(2):
            wide = x_ref[0, :, h * part : (h + 1) * part].astype(f32)
            scaled = (wide * gain_ref[0]).astype(bf16)
            at = slice(h * rows, (h + 1) * rows)
            gate_acc[at, :] += mm(scaled, gate_ref[...])
            up_acc[at, :] += mm(scaled, up_ref[...])
            square_acc[at, :] += jnp.sum(wide * wide, axis=1, keepdims=True)

    @pl.when(step == steps - 1)
    def _():
        inverse = lax.rsqrt(square_acc[...] / width + norm_eps)
        gate = inverse * gate_acc[...]
        up = inverse * up_acc[...]
        hidden[...] = (jax.nn.silu(gate) * up).astype(bf16)

    @pl.when(step >= steps)
    def _():
        for h in range(2):
            term = mm(hidden[h * rows : (h + 1) * rows, :], down_ref[...]).astype(bf16)
            for j in range(2):
                out_ref[j, :, h * part : (h + 1) * part] = term[:, j * part : (j + 1) * part]


def expert_layer(x, gain, gate_weights, up_weights, down_weights):
    steps, rows, wide = x.shape
    part = wide // 2
    hidden_width = gate_weights.shape[1]
    return pl.pallas_call(
        functools.partial(expert_kernel, steps),
        grid=(steps + steps // 2,),
        in_specs=[
            pl.BlockSpec((1, rows, wide), lambda s: (jnp.minimum(s, steps - 1), 0, 0)),
            pl.BlockSpec((1, 1, part), lambda s: (jnp.minimum(s, steps - 1), 0, 0)),
            pl.BlockSpec((part, hidden_width), lambda s: (jnp.minimum(s, steps - 1), 0)),
            pl.BlockSpec((part, hidden_width), lambda s: (jnp.minimum(s, steps - 1), 0)),
            pl.BlockSpec((hidden_width, wide), lambda s: (0, jnp.maximum(s - steps, 0))),
        ],
        out_specs=pl.BlockSpec((2, rows, wide), lambda s: (jnp.maximum(s - steps, 0), 0, 0)),
        out_shape=jax.ShapeDtypeStruct((steps, rows, wide), bf16),
        scratch_shapes=[
            pltpu.VMEM((2 * rows, hidden_width), f32),
            pltpu.VMEM((2 * rows, hidden_width), f32),
            pltpu.VMEM((2 * rows, 1), f32),
            pltpu.VMEM((2 * rows, hidden_width), bf16),
        ],
        name="expert_layer",
    )(x, gain.reshape(steps, 1, part), gate_weights, up_weights, down_weights)


def combine_kernel(experts, returned_ref, stream_ref, routes_ref, values_ref, out_ref):
    rows, wide = returned_ref.shape
    part = wide // 2
    half = rows // experts
    routes = routes_ref[...]
    values = values_ref[...].astype(f32)
    mix = (route_scale * values / jnp.sum(values, axis=0, keepdims=True)).astype(bf16).astype(f32)
    _, repeat, slot_rows, place, expert_row = slots_of(routes, experts, half)
    weight = jnp.zeros(expert_row.shape, f32)
    for k in range(routes.shape[0]):
        weight = weight + jnp.where(routes[k : k + 1, :] == expert_row, mix[k : k + 1, :], 0.0)
    weight_rows = mm(repeat, weight.astype(bf16))
    moe = stream_ref[...].astype(f32)
    for h in range(2):
        pick = jnp.where(slot_rows == place + h * half, weight_rows, 0.0).astype(bf16)
        moe = moe + mm(pick, returned_ref[:, h * part : (h + 1) * part], (0, 0))
    out_ref[...] = moe.astype(bf16)


def body(
    attn_out,
    out_weight,
    residual,
    norm_gain,
    gate_weights,
    up_weights,
    down_weights,
    routes,
    gate_values,
):
    tensor_count = lax.axis_size("tensor")
    dp_count = lax.axis_size("dp")
    expert_count = lax.axis_size("expert")
    own_tokens = attn_out.shape[0] // dp_count
    part = out_weight.shape[1] // tensor_count
    half = own_tokens * routes.shape[1] // expert_count // 2
    slot_rows = expert_count * half

    parts = project(attn_out, out_weight, tensor_count, dp_count)
    parts = parts.reshape(tensor_count * dp_count, own_tokens // 2, 2 * part)
    parts = lax.all_to_all(parts, ("tensor", "dp"), split_axis=0, concat_axis=0, tiled=True)

    stream, sent = pl.pallas_call(
        functools.partial(dispatch_kernel, expert_count),
        out_shape=(
            jax.ShapeDtypeStruct((own_tokens, part), bf16),
            jax.ShapeDtypeStruct((slot_rows, 2 * part), bf16),
        ),
        name="dispatch",
    )(parts, residual, routes.T)

    sent = sent.reshape(expert_count, half, 2 * part)
    received = lax.all_to_all(sent, "expert", split_axis=0, concat_axis=0, tiled=True)
    whole = lax.all_gather(received.reshape(slot_rows, 2 * part), "tensor", axis=0, tiled=True)

    term = expert_layer(
        whole.reshape(tensor_count, slot_rows, 2 * part),
        norm_gain,
        gate_weights[0],
        up_weights[0],
        down_weights[0],
    )
    summed = lax.psum_scatter(
        term.reshape(tensor_count * slot_rows, 2 * part), "tensor", scatter_dimension=0, tiled=True
    )
    returned = lax.all_to_all(
        summed.reshape(expert_count, half, 2 * part), "expert", split_axis=0, concat_axis=0, tiled=True
    )
    return pl.pallas_call(
        functools.partial(combine_kernel, expert_count),
        out_shape=jax.ShapeDtypeStruct((own_tokens, part), bf16),
        name="combine",
    )(returned.reshape(slot_rows, 2 * part), stream, routes.T, gate_values.T)


def solution(mesh):
    return jax.shard_map(
        body,
        mesh=mesh,
        in_specs=(
            P("expert", ("tensor", "dp")),
            P(("tensor", "dp"), None),
            P(("expert", "dp"), "tensor"),
            P(),
            P("expert", None, "tensor"),
            P("expert", None, "tensor"),
            P("expert", "tensor", None),
            P(("expert", "dp"), None),
            P(("expert", "dp"), None),
        ),
        out_specs=P(("expert", "dp"), "tensor"),
        check_vma=False,
    )
```

```python
import functools

import jax
import jax.numpy as jnp
from jax import lax
from jax.experimental import pallas as pl
from jax.experimental.pallas import tpu as pltpu
from jax.sharding import PartitionSpec as P


norm_eps = 1e-06
route_scale = 2.5
bf16 = jnp.bfloat16
f32 = jnp.float32


def mm(a, b, contract=(1, 0)):
    return lax.dot_general(
        a, b, (((contract[0],), (contract[1],)), ((), ())), preferred_element_type=f32
    )


def project_kernel(attn_ref, weight_ref, out_ref):
    own_half = out_ref.shape[2]
    part = out_ref.shape[3] // 2
    value = mm(attn_ref[...], weight_ref[...]).astype(bf16)
    for j in range(2):
        for d in range(out_ref.shape[1]):
            for h in range(2):
                row = (d * 2 + h) * own_half
                out_ref[j, d, :, h * part : (h + 1) * part] = value[
                    row : row + own_half, j * part : (j + 1) * part
                ]


def project(attn_out, out_weight, tensor_count, dp_count):
    rows, depth = attn_out.shape
    width = out_weight.shape[1]
    part = width // tensor_count
    own = rows // dp_count
    return pl.pallas_call(
        project_kernel,
        grid=(tensor_count // 2,),
        in_specs=[
            pl.BlockSpec((rows, depth), lambda s: (0, 0)),
            pl.BlockSpec((depth, 2 * part), lambda s: (0, s)),
        ],
        out_specs=pl.BlockSpec((2, dp_count, own // 2, 2 * part), lambda s: (s, 0, 0, 0)),
        out_shape=jax.ShapeDtypeStruct((tensor_count, dp_count, own // 2, 2 * part), bf16),
        name="project",
    )(attn_out, out_weight)


def slots_of(routes, experts, half):
    own = routes.shape[1]
    expert_row = lax.broadcasted_iota(jnp.int32, (experts, own), 0)
    named = jnp.zeros((experts, own), f32)
    for k in range(routes.shape[0]):
        named = named + jnp.where(routes[k : k + 1, :] == expert_row, 1.0, 0.0)
    before = jnp.where(
        lax.broadcasted_iota(jnp.int32, (own, own), 0)
        < lax.broadcasted_iota(jnp.int32, (own, own), 1),
        1.0,
        0.0,
    ).astype(bf16)
    slot = mm(named.astype(bf16), before)
    row = lax.broadcasted_iota(jnp.int32, (experts * half, experts), 0)
    col = lax.broadcasted_iota(jnp.int32, (experts * half, experts), 1)
    repeat = jnp.where(row // half == col, 1.0, 0.0).astype(bf16)
    slot_rows = mm(repeat, slot.astype(bf16))
    place = (lax.broadcasted_iota(jnp.int32, (experts * half, own), 0) % half).astype(f32)
    return named, repeat, slot_rows, place, expert_row


def dispatch_kernel(experts, parts_ref, residual_ref, routes_ref, stream_ref, sent_ref):
    rows, wide = sent_ref.shape
    part = wide // 2
    half = rows // experts
    total = parts_ref[0].astype(f32)
    for i in range(1, parts_ref.shape[0]):
        total = total + parts_ref[i].astype(f32)
    attn = jnp.concatenate([total[:, :part], total[:, part:]], axis=0)
    stream = (residual_ref[...].astype(f32) + attn).astype(bf16)
    stream_ref[...] = stream
    named, repeat, slot_rows, place, _ = slots_of(routes_ref[...], experts, half)
    named_rows = mm(repeat, named.astype(bf16))
    for h in range(2):
        pick = jnp.where(slot_rows == place + h * half, named_rows, 0.0).astype(bf16)
        sent_ref[:, h * part : (h + 1) * part] = mm(pick, stream).astype(bf16)


def pack_kernel(rank_ref, down_ref, *out_refs):
    count = len(out_refs)
    rows, wide = out_refs[0].shape
    part = wide // 2
    step = pl.program_id(0)
    for j in range(2):
        shift = lax.rem(2 * step + j + count - rank_ref[0], count)
        for s in range(count):

            @pl.when(shift == s)
            def _():
                for h in range(2):
                    out_refs[s][:, h * part : (h + 1) * part] = down_ref[
                        h * rows : (h + 1) * rows, j * part : (j + 1) * part
                    ]


def pack_down(down_weights, tensor_count):
    rows, width = down_weights.shape
    wide = 2 * (width // tensor_count)
    rank = lax.axis_index("tensor").astype(jnp.int32).reshape(1)
    whole = pl.BlockSpec((rows // 2, wide), lambda s, rank_ref: (0, 0))
    return pl.pallas_call(
        pack_kernel,
        grid_spec=pltpu.PrefetchScalarGridSpec(
            num_scalar_prefetch=1,
            grid=(tensor_count // 2,),
            in_specs=[pl.BlockSpec((rows, wide), lambda s, rank_ref: (0, s))],
            out_specs=[whole] * tensor_count,
        ),
        out_shape=[jax.ShapeDtypeStruct((rows // 2, wide), bf16)] * tensor_count,
        name="pack_down",
    )(rank, down_weights)


def hidden_kernel(steps, x_ref, gain_ref, gate_ref, up_ref, out_ref, gate_acc, up_acc, square_acc):
    step = pl.program_id(0)
    part = gate_ref.shape[0]
    rows = x_ref.shape[1]

    @pl.when(step == 0)
    def _():
        gate_acc[...] = jnp.zeros_like(gate_acc)
        up_acc[...] = jnp.zeros_like(up_acc)
        square_acc[...] = jnp.zeros_like(square_acc)

    for h in range(2):
        wide = x_ref[0, :, h * part : (h + 1) * part].astype(f32)
        scaled = (wide * gain_ref[0]).astype(bf16)
        at = slice(h * rows, (h + 1) * rows)
        gate_acc[at, :] += mm(scaled, gate_ref[...])
        up_acc[at, :] += mm(scaled, up_ref[...])
        square_acc[at, :] += jnp.sum(wide * wide, axis=1, keepdims=True)

    @pl.when(step == steps - 1)
    def _():
        inverse = lax.rsqrt(square_acc[...] / (part * steps) + norm_eps)
        gate = inverse * gate_acc[...]
        up = inverse * up_acc[...]
        out_ref[...] = (jax.nn.silu(gate) * up).astype(bf16)


def hidden_units(x, gain, gate_weights, up_weights):
    steps, rows, wide = x.shape
    part = wide // 2
    hidden_width = gate_weights.shape[1]
    return pl.pallas_call(
        functools.partial(hidden_kernel, steps),
        grid=(steps,),
        in_specs=[
            pl.BlockSpec((1, rows, wide), lambda s: (s, 0, 0)),
            pl.BlockSpec((1, 1, part), lambda s: (s, 0, 0)),
            pl.BlockSpec((part, hidden_width), lambda s: (s, 0)),
            pl.BlockSpec((part, hidden_width), lambda s: (s, 0)),
        ],
        out_specs=pl.BlockSpec((2 * rows, hidden_width), lambda s: (0, 0)),
        out_shape=jax.ShapeDtypeStruct((2 * rows, hidden_width), bf16),
        scratch_shapes=[
            pltpu.VMEM((2 * rows, hidden_width), f32),
            pltpu.VMEM((2 * rows, hidden_width), f32),
            pltpu.VMEM((2 * rows, 1), f32),
        ],
        name="hidden_units",
    )(x, gain.reshape(steps, 1, part), gate_weights, up_weights)


def output_kernel(rank_ref, hidden_ref, *refs):
    down_refs, out_ref = refs[:-1], refs[-1]
    count = len(down_refs)
    rows, wide = out_ref.shape
    part = wide // 2
    total = None
    for s, down_ref in enumerate(down_refs):
        down = jnp.concatenate([down_ref[:, :part], down_ref[:, part:]], axis=0)
        term = mm(hidden_ref[lax.rem(rank_ref[0] + count - s, count)], down)
        total = term if total is None else total + term
    for h in range(2):
        out_ref[:, h * part : (h + 1) * part] = total[h * rows : (h + 1) * rows, :].astype(bf16)


def expert_outputs(hidden, down):
    _, rows, _ = hidden.shape
    _, wide = down[0].shape
    rank = lax.axis_index("tensor").astype(jnp.int32).reshape(1)
    return pl.pallas_call(
        output_kernel,
        grid_spec=pltpu.PrefetchScalarGridSpec(
            num_scalar_prefetch=1,
            grid=(1,),
            in_specs=[pl.BlockSpec(hidden.shape, lambda i, rank_ref: (0, 0, 0))]
            + [pl.BlockSpec(d.shape, lambda i, rank_ref: (0, 0)) for d in down],
            out_specs=pl.BlockSpec((rows // 2, wide), lambda i, rank_ref: (0, 0)),
        ),
        out_shape=jax.ShapeDtypeStruct((rows // 2, wide), bf16),
        name="expert_outputs",
    )(rank, hidden, *down)


def combine_kernel(experts, returned_ref, stream_ref, routes_ref, values_ref, out_ref):
    rows, wide = returned_ref.shape
    part = wide // 2
    half = rows // experts
    routes = routes_ref[...]
    values = values_ref[...].astype(f32)
    mix = (route_scale * values / jnp.sum(values, axis=0, keepdims=True)).astype(bf16).astype(f32)
    _, repeat, slot_rows, place, expert_row = slots_of(routes, experts, half)
    weight = jnp.zeros(expert_row.shape, f32)
    for k in range(routes.shape[0]):
        weight = weight + jnp.where(routes[k : k + 1, :] == expert_row, mix[k : k + 1, :], 0.0)
    weight_rows = mm(repeat, weight.astype(bf16))
    moe = stream_ref[...].astype(f32)
    for h in range(2):
        pick = jnp.where(slot_rows == place + h * half, weight_rows, 0.0).astype(bf16)
        moe = moe + mm(pick, returned_ref[:, h * part : (h + 1) * part], (0, 0))
    out_ref[...] = moe.astype(bf16)


def body(
    attn_out,
    out_weight,
    residual,
    norm_gain,
    gate_weights,
    up_weights,
    down_weights,
    routes,
    gate_values,
):
    tensor_count = lax.axis_size("tensor")
    dp_count = lax.axis_size("dp")
    expert_count = lax.axis_size("expert")
    own_tokens = attn_out.shape[0] // dp_count
    part = out_weight.shape[1] // tensor_count
    half = own_tokens * routes.shape[1] // expert_count // 2
    slot_rows = expert_count * half

    parts = project(attn_out, out_weight, tensor_count, dp_count)
    parts = parts.reshape(tensor_count * dp_count, own_tokens // 2, 2 * part)
    parts = lax.all_to_all(parts, ("tensor", "dp"), split_axis=0, concat_axis=0, tiled=True)
    packed = pack_down(down_weights[0], tensor_count)
    stream, sent = pl.pallas_call(
        functools.partial(dispatch_kernel, expert_count),
        out_shape=(
            jax.ShapeDtypeStruct((own_tokens, part), bf16),
            jax.ShapeDtypeStruct((slot_rows, 2 * part), bf16),
        ),
        name="dispatch",
    )(parts, residual, routes.T)

    sent = sent.reshape(expert_count, half, 2 * part)
    sent, *packed = lax.optimization_barrier((sent, *packed))
    received = lax.all_to_all(sent, "expert", split_axis=0, concat_axis=0, tiled=True)
    rolled = [
        lax.ppermute(piece, "tensor", [(i, (i + shift) % tensor_count) for i in range(tensor_count)])
        if shift
        else piece
        for shift, piece in enumerate(packed)
    ]
    whole = lax.all_gather(received.reshape(slot_rows, 2 * part), "tensor", axis=0, tiled=True)

    hidden = hidden_units(
        whole.reshape(tensor_count, slot_rows, 2 * part),
        norm_gain,
        gate_weights[0],
        up_weights[0],
    )
    hidden_all = lax.all_gather(hidden, "tensor", axis=0, tiled=False)
    summed = expert_outputs(hidden_all, rolled)
    returned = lax.all_to_all(
        summed.reshape(expert_count, half, 2 * part), "expert", split_axis=0, concat_axis=0, tiled=True
    )
    return pl.pallas_call(
        functools.partial(combine_kernel, expert_count),
        out_shape=jax.ShapeDtypeStruct((own_tokens, part), bf16),
        name="combine",
    )(returned.reshape(slot_rows, 2 * part), stream, routes.T, gate_values.T)


def solution(mesh):
    return jax.shard_map(
        body,
        mesh=mesh,
        in_specs=(
            P("expert", ("tensor", "dp")),
            P(("tensor", "dp"), None),
            P(("expert", "dp"), "tensor"),
            P(),
            P("expert", None, "tensor"),
            P("expert", None, "tensor"),
            P("expert", "tensor", None),
            P(("expert", "dp"), None),
            P(("expert", "dp"), None),
        ),
        out_specs=P(("expert", "dp"), "tensor"),
        check_vma=False,
    )
```

```python
import functools

import jax
import jax.numpy as jnp
from jax import lax
from jax.experimental import pallas as pl
from jax.experimental.pallas import tpu as pltpu
from jax.sharding import PartitionSpec as P

norm_eps = 1e-06
route_scale = 2.5
bf16 = jnp.bfloat16
f32 = jnp.float32


def mm(a, b, contract=(1, 0)):
    return lax.dot_general(
        a, b, (((contract[0],), (contract[1],)), ((), ())), preferred_element_type=f32
    )


def project_kernel(attn_ref, weight_ref, out_ref):
    own_half = out_ref.shape[2]
    part = out_ref.shape[3] // 2
    value = mm(attn_ref[...], weight_ref[...]).astype(bf16)
    for j in range(2):
        for d in range(out_ref.shape[1]):
            for h in range(2):
                row = (d * 2 + h) * own_half
                out_ref[j, d, :, h * part : (h + 1) * part] = value[
                    row : row + own_half, j * part : (j + 1) * part
                ]


def project(attn_out, out_weight, tensor_count, dp_count):
    rows, depth = attn_out.shape
    width = out_weight.shape[1]
    part = width // tensor_count
    own = rows // dp_count
    return pl.pallas_call(
        project_kernel,
        grid=(tensor_count // 2,),
        in_specs=[
            pl.BlockSpec((rows, depth), lambda s: (0, 0)),
            pl.BlockSpec((depth, 2 * part), lambda s: (0, s)),
        ],
        out_specs=pl.BlockSpec((2, dp_count, own // 2, 2 * part), lambda s: (s, 0, 0, 0)),
        out_shape=jax.ShapeDtypeStruct((tensor_count, dp_count, own // 2, 2 * part), bf16),
        name="project",
    )(attn_out, out_weight)


def slots_of(routes, experts):
    own = routes.shape[1]
    expert_row = lax.broadcasted_iota(jnp.int32, (experts, own), 0)
    named = jnp.zeros((experts, own), f32)
    for k in range(routes.shape[0]):
        named = named + jnp.where(routes[k : k + 1, :] == expert_row, 1.0, 0.0)
    before = jnp.where(
        lax.broadcasted_iota(jnp.int32, (own, own), 0)
        < lax.broadcasted_iota(jnp.int32, (own, own), 1),
        1.0,
        0.0,
    ).astype(bf16)
    return named, mm(named.astype(bf16), before), expert_row


def dispatch_kernel(parts_ref, residual_ref, routes_ref, stream_ref, *sent_refs):
    part = stream_ref.shape[1]
    total = parts_ref[0].astype(f32)
    for i in range(1, parts_ref.shape[0]):
        total = total + parts_ref[i].astype(f32)
    attn = jnp.concatenate([total[:, :part], total[:, part:]], axis=0)
    stream = (residual_ref[...].astype(f32) + attn).astype(bf16)
    stream_ref[...] = stream
    named, slot, _ = slots_of(routes_ref[...], sent_refs[0].shape[0])
    first = 0
    for sent_ref in sent_refs:
        for g in range(sent_ref.shape[1] // part):
            pick = jnp.where(slot == first, named, 0.0).astype(bf16)
            sent_ref[:, g * part : (g + 1) * part] = mm(pick, stream).astype(bf16)
            first += 1


def expert_kernel(steps, x_ref, gain_ref, gate_ref, up_ref, down_ref, out_ref, gate_acc, up_acc, square_acc, hidden):
    step = pl.program_id(0)
    slices, _, part = gain_ref.shape
    rows = x_ref.shape[1]
    segments = x_ref.shape[2] // part
    width = part * slices * steps
    lanes = square_acc.shape[1]

    @pl.when(step < steps)
    def _():
        gate = up = None
        square = [None] * segments
        for k in range(slices):
            scaled = []
            for g in range(segments):
                wide = x_ref[k, :, g * part : (g + 1) * part].astype(f32)
                scaled.append((wide * gain_ref[k]).astype(bf16))
                powers = wide * wide
                for c in range(0, part, lanes):
                    piece = powers[:, c : c + lanes]
                    if piece.shape[1] < lanes:
                        piece = jnp.concatenate(
                            [piece, jnp.zeros((rows, lanes - piece.shape[1]), f32)], axis=1
                        )
                    square[g] = piece if square[g] is None else square[g] + piece
            scaled = jnp.concatenate(scaled, axis=0)
            depth = slice(k * part, (k + 1) * part)
            gate_term = mm(scaled, gate_ref[depth, :])
            up_term = mm(scaled, up_ref[depth, :])
            gate = gate_term if gate is None else gate + gate_term
            up = up_term if up is None else up + up_term
        square = jnp.concatenate(square, axis=0)

        @pl.when(step == 0)
        def _():
            gate_acc[...] = gate
            up_acc[...] = up
            square_acc[...] = square

        @pl.when(step > 0)
        def _():
            gate_acc[...] += gate
            up_acc[...] += up
            square_acc[...] += square

    @pl.when(step == steps - 1)
    def _():
        mean = jnp.sum(square_acc[...], axis=1, keepdims=True) / width
        inverse = lax.rsqrt(mean + norm_eps)
        gate = inverse * gate_acc[...]
        up = inverse * up_acc[...]
        hidden[...] = (jax.nn.silu(gate) * up).astype(bf16)

    @pl.when(step >= steps)
    def _():
        for j in range(0, out_ref.shape[0], 2):
            term = mm(hidden[...], down_ref[:, j * part : (j + 2) * part]).astype(bf16)
            for g in range(segments):
                for i in range(2):
                    out_ref[j + i, :, g * part : (g + 1) * part] = term[
                        g * rows : (g + 1) * rows, i * part : (i + 1) * part
                    ]


def expert_layer(x, gain, gate_weights, up_weights, down_weights):
    count, rows, wide = x.shape
    width, hidden_width = gate_weights.shape
    part = width // count
    total_rows = rows * (wide // part)
    slices, outs = 2, 4
    steps = count // slices

    def late(s):
        return jnp.maximum(s - steps, 0)

    return pl.pallas_call(
        functools.partial(expert_kernel, steps),
        grid=(steps + count // outs,),
        in_specs=[
            pl.BlockSpec((slices, rows, wide), lambda s: (jnp.minimum(s, steps - 1), 0, 0)),
            pl.BlockSpec((slices, 1, part), lambda s: (jnp.minimum(s, steps - 1), 0, 0)),
            pl.BlockSpec((slices * part, hidden_width), lambda s: (jnp.minimum(s, steps - 1), 0)),
            pl.BlockSpec((slices * part, hidden_width), lambda s: (jnp.minimum(s, steps - 1), 0)),
            pl.BlockSpec((hidden_width, outs * part), lambda s: (0, late(s))),
        ],
        out_specs=pl.BlockSpec((outs, rows, wide), lambda s: (late(s), 0, 0)),
        out_shape=jax.ShapeDtypeStruct((count, rows, wide), bf16),
        scratch_shapes=[
            pltpu.VMEM((total_rows, hidden_width), f32),
            pltpu.VMEM((total_rows, hidden_width), f32),
            pltpu.VMEM((total_rows, 128), f32),
            pltpu.VMEM((total_rows, hidden_width), bf16),
        ],
        name="expert_layer",
    )(x, gain.reshape(count, 1, part), gate_weights, up_weights, down_weights)


def combine_kernel(stream_ref, routes_ref, values_ref, *refs):
    returned_refs, out_ref = refs[:-1], refs[-1]
    part = stream_ref.shape[1]
    routes = routes_ref[...]
    values = values_ref[...].astype(f32)
    mix = (route_scale * values / jnp.sum(values, axis=0, keepdims=True)).astype(bf16).astype(f32)
    _, slot, expert_row = slots_of(routes, returned_refs[0].shape[0])
    weight = jnp.zeros(expert_row.shape, f32)
    for k in range(routes.shape[0]):
        weight = weight + jnp.where(routes[k : k + 1, :] == expert_row, mix[k : k + 1, :], 0.0)
    moe = stream_ref[...].astype(f32)
    first = 0
    for returned_ref in returned_refs:
        for g in range(returned_ref.shape[1] // part):
            pick = jnp.where(slot == first, weight, 0.0).astype(bf16)
            moe = moe + mm(pick, returned_ref[:, g * part : (g + 1) * part], (0, 0))
            first += 1
    out_ref[...] = moe.astype(bf16)


def swap(x, axis):
    return lax.all_to_all(x, axis, split_axis=0, concat_axis=0, tiled=True)


def body(
    attn_out,
    out_weight,
    residual,
    norm_gain,
    gate_weights,
    up_weights,
    down_weights,
    routes,
    gate_values,
):
    tensor_count = lax.axis_size("tensor")
    dp_count = lax.axis_size("dp")
    expert_count = lax.axis_size("expert")
    own_tokens = attn_out.shape[0] // dp_count
    part = out_weight.shape[1] // tensor_count
    capacity = own_tokens * routes.shape[1] // expert_count
    few = capacity // 4
    wide_a, wide_b = (capacity - few) * part, few * part
    weights = (norm_gain, gate_weights[0], up_weights[0], down_weights[0])

    def to_experts(sent):
        pairs = sent.reshape(expert_count, 2, sent.shape[1] // 2)
        return swap(pairs, "expert").reshape(sent.shape)

    parts = project(attn_out, out_weight, tensor_count, dp_count)
    parts = swap(parts.reshape(tensor_count * dp_count, own_tokens // 2, 2 * part), ("tensor", "dp"))
    stream, sent_a, sent_b = pl.pallas_call(
        dispatch_kernel,
        out_shape=(
            jax.ShapeDtypeStruct((own_tokens, part), bf16),
            jax.ShapeDtypeStruct((expert_count, wide_a), bf16),
            jax.ShapeDtypeStruct((expert_count, wide_b), bf16),
        ),
        name="dispatch",
    )(parts, residual, routes.T)

    rows_a = to_experts(sent_a)
    rows_a, sent_b = lax.optimization_barrier((rows_a, sent_b))
    whole_a = lax.all_gather(rows_a, "tensor", axis=0, tiled=False)
    rows_b = to_experts(sent_b)
    copies_b = lax.optimization_barrier(
        jnp.broadcast_to(rows_b[None], (tensor_count, *rows_b.shape))
    )
    whole_b = swap(copies_b, "tensor")
    whole_a, whole_b = lax.optimization_barrier((whole_a, whole_b))

    term_a = expert_layer(whole_a, *weights)
    term_a, whole_b = lax.optimization_barrier((term_a, whole_b))
    summed_a = lax.psum_scatter(term_a, "tensor", scatter_dimension=0, tiled=False)
    term_b = swap(expert_layer(whole_b, *weights), "tensor")
    summed_b = jnp.sum(term_b.astype(f32), axis=0).astype(bf16)
    returned_b = to_experts(summed_b)
    summed_a, returned_b = lax.optimization_barrier((summed_a, returned_b))
    returned_a = to_experts(summed_a)
    return pl.pallas_call(
        combine_kernel,
        out_shape=jax.ShapeDtypeStruct((own_tokens, part), bf16),
        name="combine",
    )(stream, routes.T, gate_values.T, returned_a, returned_b)


def solution(mesh):
    return jax.shard_map(
        body,
        mesh=mesh,
        in_specs=(
            P("expert", ("tensor", "dp")),
            P(("tensor", "dp"), None),
            P(("expert", "dp"), "tensor"),
            P(),
            P("expert", None, "tensor"),
            P("expert", None, "tensor"),
            P("expert", "tensor", None),
            P(("expert", "dp"), None),
            P(("expert", "dp"), None),
        ),
        out_specs=P(("expert", "dp"), "tensor"),
        check_vma=False,
    )
```

```python
import functools

import jax
import jax.numpy as jnp
from jax import lax
from jax.experimental import pallas as pl
from jax.experimental.pallas import tpu as pltpu
from jax.sharding import PartitionSpec as P

norm_eps = 1e-06
route_scale = 2.5
bf16 = jnp.bfloat16
f32 = jnp.float32


def mm(a, b, contract=(1, 0)):
    return lax.dot_general(
        a, b, (((contract[0],), (contract[1],)), ((), ())), preferred_element_type=f32
    )


def project_kernel(attn_ref, weight_ref, out_ref):
    own_half = out_ref.shape[2]
    part = out_ref.shape[3] // 2
    value = mm(attn_ref[...], weight_ref[...]).astype(bf16)
    for j in range(2):
        for d in range(out_ref.shape[1]):
            for h in range(2):
                row = (d * 2 + h) * own_half
                out_ref[j, d, :, h * part : (h + 1) * part] = value[
                    row : row + own_half, j * part : (j + 1) * part
                ]


def project(attn_out, out_weight, tensor_count, dp_count):
    rows, depth = attn_out.shape
    width = out_weight.shape[1]
    part = width // tensor_count
    own = rows // dp_count
    return pl.pallas_call(
        project_kernel,
        grid=(tensor_count // 2,),
        in_specs=[
            pl.BlockSpec((rows, depth), lambda s: (0, 0)),
            pl.BlockSpec((depth, 2 * part), lambda s: (0, s)),
        ],
        out_specs=pl.BlockSpec((2, dp_count, own // 2, 2 * part), lambda s: (s, 0, 0, 0)),
        out_shape=jax.ShapeDtypeStruct((tensor_count, dp_count, own // 2, 2 * part), bf16),
        compiler_params=pltpu.CompilerParams(vmem_limit_bytes=16 << 20),
        name="project",
    )(attn_out, in_hbm(out_weight))


def slots_of(routes, experts):
    own = routes.shape[1]
    expert_row = lax.broadcasted_iota(jnp.int32, (experts, own), 0)
    named = jnp.zeros((experts, own), f32)
    for k in range(routes.shape[0]):
        named = named + jnp.where(routes[k : k + 1, :] == expert_row, 1.0, 0.0)
    before = jnp.where(
        lax.broadcasted_iota(jnp.int32, (own, own), 0)
        < lax.broadcasted_iota(jnp.int32, (own, own), 1),
        1.0,
        0.0,
    ).astype(bf16)
    return named, mm(named.astype(bf16), before), expert_row


def dispatch_kernel(parts_ref, residual_ref, routes_ref, stream_ref, sent_ref):
    part = stream_ref.shape[1]
    total = parts_ref[0].astype(f32)
    for i in range(1, parts_ref.shape[0]):
        total = total + parts_ref[i].astype(f32)
    attn = jnp.concatenate([total[:, :part], total[:, part:]], axis=0)
    stream = (residual_ref[...].astype(f32) + attn).astype(bf16)
    stream_ref[...] = stream
    named, slot, _ = slots_of(routes_ref[...], sent_ref.shape[0])
    segments = sent_ref.shape[2] // part
    for g in range(segments):
        lines = []
        for i in range(2):
            pick = jnp.where(slot == i * segments + g, named, 0.0).astype(bf16)
            lines.append(mm(pick, stream)[:, None, :])
        sent_ref[:, :, g * part : (g + 1) * part] = jnp.concatenate(lines, axis=1).astype(bf16)


def expert_kernel(steps, x_ref, gain_ref, gate_ref, up_ref, down_ref, out_ref, gate_acc, up_acc, square_acc, hidden):
    step = pl.program_id(0)
    slices, _, part = gain_ref.shape
    rows = x_ref.shape[1]
    segments = x_ref.shape[2] // part
    width = part * slices * steps
    lanes = square_acc.shape[1]

    @pl.when(step < steps)
    def _():
        gate = up = None
        square = [None] * segments
        for k in range(slices):
            scaled = []
            for g in range(segments):
                wide = x_ref[k, :, g * part : (g + 1) * part].astype(f32)
                scaled.append((wide * gain_ref[k]).astype(bf16))
                powers = wide * wide
                for c in range(0, part, lanes):
                    piece = powers[:, c : c + lanes]
                    if piece.shape[1] < lanes:
                        piece = jnp.concatenate(
                            [piece, jnp.zeros((rows, lanes - piece.shape[1]), f32)], axis=1
                        )
                    square[g] = piece if square[g] is None else square[g] + piece
            scaled = jnp.concatenate(scaled, axis=0)
            depth = slice(k * part, (k + 1) * part)
            whole_depth = pl.ds(pl.multiple_of((step * slices + k) * part, 64), part)
            gate_term = mm(scaled, gate_ref[whole_depth, :])
            up_term = mm(scaled, up_ref[depth, :])
            gate = gate_term if gate is None else gate + gate_term
            up = up_term if up is None else up + up_term
        square = jnp.concatenate(square, axis=0)

        @pl.when(step == 0)
        def _():
            gate_acc[...] = gate
            up_acc[...] = up
            square_acc[...] = square

        @pl.when(step > 0)
        def _():
            gate_acc[...] += gate
            up_acc[...] += up
            square_acc[...] += square

    @pl.when(step == steps - 1)
    def _():
        mean = jnp.sum(square_acc[...], axis=1, keepdims=True) / width
        inverse = lax.rsqrt(mean + norm_eps)
        gate = inverse * gate_acc[...]
        up = inverse * up_acc[...]
        hidden[...] = (jax.nn.silu(gate) * up).astype(bf16)

    @pl.when(step >= steps)
    def _():
        for j in range(0, out_ref.shape[0], 2):
            term = mm(hidden[...], down_ref[:, j * part : (j + 2) * part]).astype(bf16)
            for g in range(segments):
                for i in range(2):
                    out_ref[j + i, :, g * part : (g + 1) * part] = term[
                        g * rows : (g + 1) * rows, i * part : (i + 1) * part
                    ]


def expert_layer(x, gain, gate_weights, up_weights, down_weights):
    count, rows, wide = x.shape
    width, hidden_width = gate_weights.shape
    part = width // count
    total_rows = rows * (wide // part)
    slices, outs = 2, 4
    steps = count // slices

    def late(s):
        return jnp.maximum(s - steps, 0)

    return pl.pallas_call(
        functools.partial(expert_kernel, steps),
        grid=(steps + count // outs,),
        in_specs=[
            pl.BlockSpec((slices, rows, wide), lambda s: (jnp.minimum(s, steps - 1), 0, 0)),
            pl.BlockSpec((slices, 1, part), lambda s: (jnp.minimum(s, steps - 1), 0, 0)),
            pl.BlockSpec(memory_space=pltpu.VMEM),
            pl.BlockSpec((slices * part, hidden_width), lambda s: (jnp.minimum(s, steps - 1), 0)),
            pl.BlockSpec((hidden_width, outs * part), lambda s: (0, late(s))),
        ],
        out_specs=pl.BlockSpec((outs, rows, wide), lambda s: (late(s), 0, 0)),
        out_shape=pltpu.HBM((count, rows, wide), bf16),
        scratch_shapes=[
            pltpu.VMEM((total_rows, hidden_width), f32),
            pltpu.VMEM((total_rows, hidden_width), f32),
            pltpu.VMEM((total_rows, 128), f32),
            pltpu.VMEM((total_rows, hidden_width), bf16),
        ],
        compiler_params=pltpu.CompilerParams(vmem_limit_bytes=28 << 20),
        name="expert_layer",
    )(x, gain.reshape(count, 1, part), gate_weights, up_weights, down_weights)


def combine_kernel(stream_ref, routes_ref, values_ref, returned_ref, out_ref):
    part = stream_ref.shape[1]
    routes = routes_ref[...]
    values = values_ref[...].astype(f32)
    mix = (route_scale * values / jnp.sum(values, axis=0, keepdims=True)).astype(bf16).astype(f32)
    _, slot, expert_row = slots_of(routes, returned_ref.shape[0])
    weight = jnp.zeros(expert_row.shape, f32)
    for k in range(routes.shape[0]):
        weight = weight + jnp.where(routes[k : k + 1, :] == expert_row, mix[k : k + 1, :], 0.0)
    moe = stream_ref[...].astype(f32)
    segments = returned_ref.shape[2] // part
    for g in range(segments):
        pair = returned_ref[:, :, g * part : (g + 1) * part].astype(f32)
        for i in range(2):
            pick = jnp.where(slot == i * segments + g, weight, 0.0).astype(bf16)
            moe = moe + mm(pick, pair[:, i, :].astype(bf16), (0, 0))
    out_ref[...] = moe.astype(bf16)


def in_hbm(x):
    return pltpu.with_memory_space_constraint(x, pltpu.HBM)


def swap(x, axis):
    return lax.all_to_all(x, axis, split_axis=0, concat_axis=0, tiled=True)


def body(
    attn_out,
    out_weight,
    residual,
    norm_gain,
    gate_weights,
    up_weights,
    down_weights,
    routes,
    gate_values,
):
    tensor_count = lax.axis_size("tensor")
    dp_count = lax.axis_size("dp")
    expert_count = lax.axis_size("expert")
    own_tokens = attn_out.shape[0] // dp_count
    part = out_weight.shape[1] // tensor_count
    capacity = own_tokens * routes.shape[1] // expert_count

    parts = project(attn_out, out_weight, tensor_count, dp_count)
    parts = swap(parts.reshape(tensor_count * dp_count, own_tokens // 2, 2 * part), ("tensor", "dp"))
    stream, sent = pl.pallas_call(
        dispatch_kernel,
        out_shape=(
            jax.ShapeDtypeStruct((own_tokens, part), bf16),
            jax.ShapeDtypeStruct((expert_count, 2, capacity // 2 * part), bf16),
        ),
        compiler_params=pltpu.CompilerParams(vmem_limit_bytes=16 << 20),
        name="dispatch",
    )(parts, residual, routes.T)

    whole = lax.all_gather(
        swap(sent, "expert").reshape(expert_count, capacity * part), "tensor", axis=0, tiled=False)
    term = expert_layer(
        in_hbm(whole),
        norm_gain,
        pltpu.with_memory_space_constraint(gate_weights[0], pltpu.VMEM),
        in_hbm(up_weights[0]),
        in_hbm(down_weights[0]),
    )
    summed = lax.psum_scatter(term, "tensor", scatter_dimension=0, tiled=False)
    returned = swap(summed.reshape(expert_count, 2, capacity // 2 * part), "expert")
    return pl.pallas_call(
        combine_kernel,
        out_shape=jax.ShapeDtypeStruct((own_tokens, part), bf16),
        compiler_params=pltpu.CompilerParams(vmem_limit_bytes=16 << 20),
        name="combine",
    )(stream, routes.T, gate_values.T, returned)


def solution(mesh):
    return jax.shard_map(
        body,
        mesh=mesh,
        in_specs=(
            P("expert", ("tensor", "dp")),
            P(("tensor", "dp"), None),
            P(("expert", "dp"), "tensor"),
            P(),
            P("expert", None, "tensor"),
            P("expert", None, "tensor"),
            P("expert", "tensor", None),
            P(("expert", "dp"), None),
            P(("expert", "dp"), None),
        ),
        out_specs=P(("expert", "dp"), "tensor"),
        check_vma=False,
    )
```

```python
import functools

import jax
import jax.numpy as jnp
from jax import lax
from jax.experimental import pallas as pl
from jax.experimental.pallas import tpu as pltpu
from jax.sharding import PartitionSpec as P


norm_eps = 1e-06
route_scale = 2.5
bf16 = jnp.bfloat16
f32 = jnp.float32


def mm(a, b, contract=(1, 0)):
    return lax.dot_general(
        a, b, (((contract[0],), (contract[1],)), ((), ())), preferred_element_type=f32
    )


def project_kernel(attn_ref, weight_ref, out_ref):
    own_half = out_ref.shape[2]
    part = out_ref.shape[3] // 2
    value = mm(attn_ref[...], weight_ref[...]).astype(bf16)
    for j in range(2):
        for d in range(out_ref.shape[1]):
            for h in range(2):
                row = (d * 2 + h) * own_half
                out_ref[j, d, :, h * part : (h + 1) * part] = value[
                    row : row + own_half, j * part : (j + 1) * part
                ]


def project(attn_out, out_weight, tensor_count, dp_count):
    rows, depth = attn_out.shape
    width = out_weight.shape[1]
    part = width // tensor_count
    own = rows // dp_count
    return pl.pallas_call(
        project_kernel,
        grid=(tensor_count // 2,),
        in_specs=[
            pl.BlockSpec((rows, depth), lambda s: (0, 0)),
            pl.BlockSpec((depth, 2 * part), lambda s: (0, s)),
        ],
        out_specs=pl.BlockSpec((2, dp_count, own // 2, 2 * part), lambda s: (s, 0, 0, 0)),
        out_shape=jax.ShapeDtypeStruct((tensor_count, dp_count, own // 2, 2 * part), bf16),
        compiler_params=pltpu.CompilerParams(vmem_limit_bytes=16 << 20),
        name="project",
    )(attn_out, in_hbm(out_weight))


def slots_of(routes, experts):
    own = routes.shape[1]
    expert_row = lax.broadcasted_iota(jnp.int32, (experts, own), 0)
    named = jnp.zeros((experts, own), f32)
    for k in range(routes.shape[0]):
        named = named + jnp.where(routes[k : k + 1, :] == expert_row, 1.0, 0.0)
    before = jnp.where(
        lax.broadcasted_iota(jnp.int32, (own, own), 0)
        < lax.broadcasted_iota(jnp.int32, (own, own), 1),
        1.0,
        0.0,
    ).astype(bf16)
    return named, mm(named.astype(bf16), before), expert_row


def dispatch_kernel(parts_ref, residual_ref, routes_ref, stream_ref, sent_ref):
    part = stream_ref.shape[1]
    total = parts_ref[0].astype(f32)
    for i in range(1, parts_ref.shape[0]):
        total = total + parts_ref[i].astype(f32)
    attn = jnp.concatenate([total[:, :part], total[:, part:]], axis=0)
    stream = (residual_ref[...].astype(f32) + attn).astype(bf16)
    stream_ref[...] = stream
    named, slot, _ = slots_of(routes_ref[...], sent_ref.shape[0])
    segments = sent_ref.shape[2] // part
    for g in range(segments):
        lines = []
        for i in range(2):
            pick = jnp.where(slot == i * segments + g, named, 0.0).astype(bf16)
            lines.append(mm(pick, stream)[:, None, :])
        sent_ref[:, :, g * part : (g + 1) * part] = jnp.concatenate(lines, axis=1).astype(bf16)


def pack_kernel(rank_ref, down_ref, *out_refs):
    count = len(out_refs)
    rows, wide = out_refs[0].shape
    part = wide // 2
    step = pl.program_id(0)
    for j in range(2):
        shift = lax.rem(2 * step + j + count - rank_ref[0], count)
        for s in range(count):

            @pl.when(shift == s)
            def _():
                for h in range(2):
                    out_refs[s][:, h * part : (h + 1) * part] = down_ref[
                        h * rows : (h + 1) * rows, j * part : (j + 1) * part
                    ]


def pack_down(down_weights, tensor_count, dp_count):
    rows, width = down_weights.shape[0] // dp_count, down_weights.shape[1]
    wide = 2 * (width // tensor_count)
    rank = jnp.stack([lax.axis_index("tensor"), lax.axis_index("dp")]).astype(jnp.int32)
    whole = pl.BlockSpec((rows // 2, wide), lambda s, rank_ref: (0, 0))
    return pl.pallas_call(
        pack_kernel,
        grid_spec=pltpu.PrefetchScalarGridSpec(
            num_scalar_prefetch=1,
            grid=(tensor_count // 2,),
            in_specs=[pl.BlockSpec((rows, wide), lambda s, rank_ref: (rank_ref[1], s))],
            out_specs=[whole] * tensor_count,
        ),
        out_shape=[jax.ShapeDtypeStruct((rows // 2, wide), bf16)] * tensor_count,
        compiler_params=pltpu.CompilerParams(vmem_limit_bytes=16 << 20),
        name="pack_down",
    )(rank, in_hbm(down_weights))


def hidden_kernel(steps, x_ref, gain_ref, gate_ref, up_ref, out_ref, gate_acc, up_acc, square_acc):
    step = pl.program_id(0)
    slices, _, part = gain_ref.shape
    rows = x_ref.shape[1]
    segments = x_ref.shape[2] // part
    width = part * slices * steps
    lanes = square_acc.shape[1]
    gate = up = None
    square = [None] * segments
    for k in range(slices):
        scaled = []
        for g in range(segments):
            wide = x_ref[k, :, g * part : (g + 1) * part].astype(f32)
            scaled.append((wide * gain_ref[k]).astype(bf16))
            powers = wide * wide
            for c in range(0, part, lanes):
                piece = powers[:, c : c + lanes]
                if piece.shape[1] < lanes:
                    piece = jnp.concatenate(
                        [piece, jnp.zeros((rows, lanes - piece.shape[1]), f32)], axis=1
                    )
                square[g] = piece if square[g] is None else square[g] + piece
        scaled = jnp.concatenate(scaled, axis=0)
        depth = slice(k * part, (k + 1) * part)
        whole_depth = pl.ds(pl.multiple_of((step * slices + k) * part, 64), part)
        gate_term = mm(scaled, gate_ref[whole_depth, :])
        up_term = mm(scaled, up_ref[depth, :])
        gate = gate_term if gate is None else gate + gate_term
        up = up_term if up is None else up + up_term
    square = jnp.concatenate(square, axis=0)

    @pl.when(step == 0)
    def _():
        gate_acc[...] = gate
        up_acc[...] = up
        square_acc[...] = square

    @pl.when(step > 0)
    def _():
        gate_acc[...] += gate
        up_acc[...] += up
        square_acc[...] += square

    @pl.when(step == steps - 1)
    def _():
        mean = jnp.sum(square_acc[...], axis=1, keepdims=True) / width
        inverse = lax.rsqrt(mean + norm_eps)
        gate = inverse * gate_acc[...]
        up = inverse * up_acc[...]
        out_ref[...] = (jax.nn.silu(gate) * up).astype(bf16)


def hidden_units(x, gain, gate_weights, up_weights):
    count, rows, wide = x.shape
    width, hidden_width = gate_weights.shape
    part = width // count
    total_rows = rows * (wide // part)
    slices = 2
    steps = count // slices
    return pl.pallas_call(
        functools.partial(hidden_kernel, steps),
        grid=(steps,),
        in_specs=[
            pl.BlockSpec((slices, rows, wide), lambda s: (s, 0, 0)),
            pl.BlockSpec((slices, 1, part), lambda s: (s, 0, 0)),
            pl.BlockSpec(memory_space=pltpu.VMEM),
            pl.BlockSpec((slices * part, hidden_width), lambda s: (s, 0)),
        ],
        out_specs=pl.BlockSpec((total_rows, hidden_width), lambda s: (0, 0)),
        out_shape=pltpu.HBM((total_rows, hidden_width), bf16),
        scratch_shapes=[
            pltpu.VMEM((total_rows, hidden_width), f32),
            pltpu.VMEM((total_rows, hidden_width), f32),
            pltpu.VMEM((total_rows, 128), f32),
        ],
        compiler_params=pltpu.CompilerParams(vmem_limit_bytes=28 << 20),
        name="hidden_units",
    )(x, gain.reshape(count, 1, part), gate_weights, up_weights)


def output_kernel(steps, rank_ref, first_ref, second_ref, low_ref, high_ref, out_ref, acc):
    step = pl.program_id(0)
    rows = out_ref.shape[0]
    part = acc.shape[1]
    segments = out_ref.shape[2] // part
    total = None
    for k, hidden_ref in enumerate((first_ref, second_ref)):
        down = jnp.concatenate(
            [
                ref[k, :, h * part : (h + 1) * part]
                for ref in (low_ref, high_ref)
                for h in range(2)
            ],
            axis=0,
        )
        term = mm(hidden_ref[0], down)
        total = term if total is None else total + term

    @pl.when(step == 0)
    def _():
        acc[...] = total

    @pl.when(step > 0)
    def _():
        acc[...] += total

    @pl.when(step == steps - 1)
    def _():
        for g in range(segments):
            lines = [
                acc[(i * segments + g) * rows : (i * segments + g + 1) * rows, :][:, None, :]
                for i in range(2)
            ]
            out_ref[:, :, g * part : (g + 1) * part] = jnp.concatenate(lines, axis=1).astype(bf16)


def expert_outputs(hidden, low, high, out_rows):
    count, total_rows, depth = hidden.shape
    _, quarter, wide = low.shape
    part = wide // 2
    steps = count // 2
    rank = lax.axis_index("tensor").astype(jnp.int32).reshape(1)
    half_wide = total_rows // out_rows // 2 * part

    def block(k):
        return pl.BlockSpec(
            (1, total_rows, depth),
            lambda s, rank_ref: (lax.rem(rank_ref[0] + count - (2 * s + k), count), 0, 0),
        )

    pieces = pl.BlockSpec((2, quarter, wide), lambda s, rank_ref: (s, 0, 0))
    return pl.pallas_call(
        functools.partial(output_kernel, steps),
        grid_spec=pltpu.PrefetchScalarGridSpec(
            num_scalar_prefetch=1,
            grid=(steps,),
            in_specs=[block(0), block(1), pieces, pieces],
            out_specs=pl.BlockSpec((out_rows, 2, half_wide), lambda s, rank_ref: (0, 0, 0)),
            scratch_shapes=[pltpu.VMEM((total_rows, part), f32)],
        ),
        out_shape=jax.ShapeDtypeStruct((out_rows, 2, half_wide), bf16),
        compiler_params=pltpu.CompilerParams(vmem_limit_bytes=28 << 20),
        name="expert_outputs",
    )(rank, hidden, hidden, low, high)


def combine_kernel(stream_ref, routes_ref, values_ref, returned_ref, out_ref):
    part = stream_ref.shape[1]
    routes = routes_ref[...]
    values = values_ref[...].astype(f32)
    mix = (route_scale * values / jnp.sum(values, axis=0, keepdims=True)).astype(bf16).astype(f32)
    _, slot, expert_row = slots_of(routes, returned_ref.shape[0])
    weight = jnp.zeros(expert_row.shape, f32)
    for k in range(routes.shape[0]):
        weight = weight + jnp.where(routes[k : k + 1, :] == expert_row, mix[k : k + 1, :], 0.0)
    moe = stream_ref[...].astype(f32)
    segments = returned_ref.shape[2] // part
    for g in range(segments):
        pair = returned_ref[:, :, g * part : (g + 1) * part].astype(f32)
        for i in range(2):
            pick = jnp.where(slot == i * segments + g, weight, 0.0).astype(bf16)
            moe = moe + mm(pick, pair[:, i, :].astype(bf16), (0, 0))
    out_ref[...] = moe.astype(bf16)


def in_hbm(x):
    return pltpu.with_memory_space_constraint(x, pltpu.HBM)


def swap(x, axis):
    return lax.all_to_all(x, axis, split_axis=0, concat_axis=0, tiled=True)


def body(
    attn_out,
    out_weight,
    residual,
    norm_gain,
    gate_weights,
    up_weights,
    down_weights,
    routes,
    gate_values,
):
    tensor_count = lax.axis_size("tensor")
    dp_count = lax.axis_size("dp")
    expert_count = lax.axis_size("expert")
    own_tokens = attn_out.shape[0] // dp_count
    part = out_weight.shape[1] // tensor_count
    capacity = own_tokens * routes.shape[1] // expert_count

    parts = project(attn_out, out_weight, tensor_count, dp_count)
    parts = swap(parts.reshape(tensor_count * dp_count, own_tokens // 2, 2 * part), ("tensor", "dp"))
    stream, sent = pl.pallas_call(
        dispatch_kernel,
        out_shape=(
            jax.ShapeDtypeStruct((own_tokens, part), bf16),
            jax.ShapeDtypeStruct((expert_count, 2, capacity // 2 * part), bf16),
        ),
        compiler_params=pltpu.CompilerParams(vmem_limit_bytes=16 << 20),
        name="dispatch",
    )(parts, residual, routes.T)

    packed = pack_down(down_weights[0], tensor_count, dp_count)
    sent, *packed = lax.optimization_barrier((sent, *packed))
    received = swap(sent, "expert")
    rolled = [
        lax.ppermute(piece, "tensor", [(i, (i + s) % tensor_count) for i in range(tensor_count)])
        if s
        else piece
        for s, piece in enumerate(packed)
    ]
    whole = lax.all_gather(
        received.reshape(expert_count, capacity * part), "tensor", axis=0, tiled=False
    )
    hidden = hidden_units(
        in_hbm(whole),
        norm_gain,
        pltpu.with_memory_space_constraint(gate_weights[0], pltpu.VMEM),
        in_hbm(up_weights[0]),
    )
    hidden_all = lax.all_gather(hidden, "tensor", axis=0, tiled=False)
    mine = jnp.stack(rolled)
    theirs = lax.ppermute(mine, "dp", [(0, 1), (1, 0)])
    first = lax.axis_index("dp") == 0
    low = jnp.where(first, mine, theirs)
    high = jnp.where(first, theirs, mine)
    returned = swap(expert_outputs(in_hbm(hidden_all), low, high, expert_count), "expert")
    return pl.pallas_call(
        combine_kernel,
        out_shape=jax.ShapeDtypeStruct((own_tokens, part), bf16),
        compiler_params=pltpu.CompilerParams(vmem_limit_bytes=16 << 20),
        name="combine",
    )(stream, routes.T, gate_values.T, returned)


def solution(mesh):
    return jax.shard_map(
        body,
        mesh=mesh,
        in_specs=(
            P("expert", ("tensor", "dp")),
            P(("tensor", "dp"), None),
            P(("expert", "dp"), "tensor"),
            P(),
            P("expert", None, "tensor"),
            P("expert", None, "tensor"),
            P("expert", "tensor", None),
            P(("expert", "dp"), None),
            P(("expert", "dp"), None),
        ),
        out_specs=P(("expert", "dp"), "tensor"),
        check_vma=False,
    )
```

```python
import functools

import jax
import jax.numpy as jnp
from jax import lax
from jax.experimental import pallas as pl
from jax.experimental.pallas import tpu as pltpu
from jax.sharding import PartitionSpec as P


norm_eps = 1e-06
route_scale = 2.5
bf16 = jnp.bfloat16
f32 = jnp.float32


def mm(a, b, contract=(1, 0)):
    return lax.dot_general(
        a, b, (((contract[0],), (contract[1],)), ((), ())), preferred_element_type=f32
    )


def project_kernel(attn_ref, weight_ref, out_ref):
    own_half = out_ref.shape[2]
    part = out_ref.shape[3] // 2
    value = mm(attn_ref[...], weight_ref[...]).astype(bf16)
    for j in range(2):
        for d in range(out_ref.shape[1]):
            for h in range(2):
                row = (d * 2 + h) * own_half
                out_ref[j, d, :, h * part : (h + 1) * part] = value[
                    row : row + own_half, j * part : (j + 1) * part
                ]


def project(attn_out, out_weight, tensor_count, dp_count):
    rows, depth = attn_out.shape
    width = out_weight.shape[1]
    part = width // tensor_count
    own = rows // dp_count
    return pl.pallas_call(
        project_kernel,
        grid=(tensor_count // 2,),
        in_specs=[
            pl.BlockSpec((rows, depth), lambda s: (0, 0)),
            pl.BlockSpec((depth, 2 * part), lambda s: (0, s)),
        ],
        out_specs=pl.BlockSpec((2, dp_count, own // 2, 2 * part), lambda s: (s, 0, 0, 0)),
        out_shape=jax.ShapeDtypeStruct((tensor_count, dp_count, own // 2, 2 * part), bf16),
        compiler_params=pltpu.CompilerParams(vmem_limit_bytes=16 << 20),
        name="project",
    )(attn_out, in_hbm(out_weight))


def slots_of(routes, experts):
    own = routes.shape[1]
    expert_row = lax.broadcasted_iota(jnp.int32, (experts, own), 0)
    named = jnp.zeros((experts, own), f32)
    for k in range(routes.shape[0]):
        named = named + jnp.where(routes[k : k + 1, :] == expert_row, 1.0, 0.0)
    before = jnp.where(
        lax.broadcasted_iota(jnp.int32, (own, own), 0)
        < lax.broadcasted_iota(jnp.int32, (own, own), 1),
        1.0,
        0.0,
    ).astype(bf16)
    return named, mm(named.astype(bf16), before), expert_row


def dispatch_kernel(parts_ref, residual_ref, routes_ref, stream_ref, sent_ref):
    part = stream_ref.shape[1]
    total = parts_ref[0].astype(f32)
    for i in range(1, parts_ref.shape[0]):
        total = total + parts_ref[i].astype(f32)
    attn = jnp.concatenate([total[:, :part], total[:, part:]], axis=0)
    stream = (residual_ref[...].astype(f32) + attn).astype(bf16)
    stream_ref[...] = stream
    named, slot, _ = slots_of(routes_ref[...], sent_ref.shape[0])
    segments = sent_ref.shape[2] // part
    for g in range(segments):
        lines = []
        for i in range(2):
            pick = jnp.where(slot == i * segments + g, named, 0.0).astype(bf16)
            lines.append(mm(pick, stream)[:, None, :])
        sent_ref[:, :, g * part : (g + 1) * part] = jnp.concatenate(lines, axis=1).astype(bf16)


def pack_kernel(rank_ref, down_ref, *out_refs):
    count = len(out_refs)
    rows, wide = out_refs[0].shape
    part = wide // 2
    step = pl.program_id(0)
    for j in range(2):
        shift = lax.rem(2 * step + j + count - rank_ref[0], count)
        for s in range(count):

            @pl.when(shift == s)
            def _():
                for h in range(2):
                    out_refs[s][:, h * part : (h + 1) * part] = down_ref[
                        h * rows : (h + 1) * rows, j * part : (j + 1) * part
                    ]


def pack_down(down_weights, tensor_count, dp_count):
    rows, width = down_weights.shape[0] // dp_count, down_weights.shape[1]
    wide = 2 * (width // tensor_count)
    rank = jnp.stack([lax.axis_index("tensor"), lax.axis_index("dp")]).astype(jnp.int32)
    whole = pl.BlockSpec((rows // 2, wide), lambda s, rank_ref: (0, 0))
    return pl.pallas_call(
        pack_kernel,
        grid_spec=pltpu.PrefetchScalarGridSpec(
            num_scalar_prefetch=1,
            grid=(tensor_count // 2,),
            in_specs=[pl.BlockSpec((rows, wide), lambda s, rank_ref: (rank_ref[1], s))],
            out_specs=[whole] * tensor_count,
        ),
        out_shape=[jax.ShapeDtypeStruct((rows // 2, wide), bf16)] * tensor_count,
        compiler_params=pltpu.CompilerParams(vmem_limit_bytes=16 << 20),
        name="pack_down",
    )(rank, in_hbm(down_weights))


def hidden_kernel(steps, x_ref, gain_ref, gate_ref, up_ref, out_ref, gate_acc, up_acc, square_acc):
    step = pl.program_id(0)
    slices, _, part = gain_ref.shape
    rows = x_ref.shape[1]
    segments = x_ref.shape[2] // part
    width = part * slices * steps
    lanes = square_acc.shape[1]
    gate = up = None
    square = [None] * segments
    for k in range(slices):
        scaled = []
        for g in range(segments):
            wide = x_ref[k, :, g * part : (g + 1) * part].astype(f32)
            scaled.append((wide * gain_ref[k]).astype(bf16))
            powers = wide * wide
            for c in range(0, part, lanes):
                piece = powers[:, c : c + lanes]
                if piece.shape[1] < lanes:
                    piece = jnp.concatenate(
                        [piece, jnp.zeros((rows, lanes - piece.shape[1]), f32)], axis=1
                    )
                square[g] = piece if square[g] is None else square[g] + piece
        scaled = jnp.concatenate(scaled, axis=0)
        depth = slice(k * part, (k + 1) * part)
        whole_depth = pl.ds(pl.multiple_of((step * slices + k) * part, 64), part)
        gate_term = mm(scaled, gate_ref[whole_depth, :])
        up_term = mm(scaled, up_ref[depth, :])
        gate = gate_term if gate is None else gate + gate_term
        up = up_term if up is None else up + up_term
    square = jnp.concatenate(square, axis=0)

    @pl.when(step == 0)
    def _():
        gate_acc[...] = gate
        up_acc[...] = up
        square_acc[...] = square

    @pl.when(step > 0)
    def _():
        gate_acc[...] += gate
        up_acc[...] += up
        square_acc[...] += square

    @pl.when(step == steps - 1)
    def _():
        mean = jnp.sum(square_acc[...], axis=1, keepdims=True) / width
        inverse = lax.rsqrt(mean + norm_eps)
        gate = inverse * gate_acc[...]
        up = inverse * up_acc[...]
        out_ref[...] = (jax.nn.silu(gate) * up).astype(bf16)


def hidden_units(x, gain, gate_weights, up_weights):
    count, rows, wide = x.shape
    width, hidden_width = gate_weights.shape
    part = width // count
    total_rows = rows * (wide // part)
    slices = 2
    steps = count // slices
    return pl.pallas_call(
        functools.partial(hidden_kernel, steps),
        grid=(steps,),
        in_specs=[
            pl.BlockSpec((slices, rows, wide), lambda s: (s, 0, 0)),
            pl.BlockSpec((slices, 1, part), lambda s: (s, 0, 0)),
            pl.BlockSpec(memory_space=pltpu.VMEM),
            pl.BlockSpec((slices * part, hidden_width), lambda s: (s, 0)),
        ],
        out_specs=pl.BlockSpec((total_rows, hidden_width), lambda s: (0, 0)),
        out_shape=pltpu.HBM((total_rows, hidden_width), bf16),
        scratch_shapes=[
            pltpu.VMEM((total_rows, hidden_width), f32),
            pltpu.VMEM((total_rows, hidden_width), f32),
            pltpu.VMEM((total_rows, 128), f32),
        ],
        compiler_params=pltpu.CompilerParams(vmem_limit_bytes=28 << 20),
        name="hidden_units",
    )(x, gain.reshape(count, 1, part), gate_weights, up_weights)


def output_kernel(steps, rank_ref, first_ref, second_ref, low_ref, high_ref, out_ref, acc):
    step = pl.program_id(0)
    rows = out_ref.shape[0]
    part = acc.shape[1]
    segments = out_ref.shape[2] // part
    total = None
    for k, hidden_ref in enumerate((first_ref, second_ref)):
        down = jnp.concatenate(
            [
                ref[k, :, h * part : (h + 1) * part]
                for ref in (low_ref, high_ref)
                for h in range(2)
            ],
            axis=0,
        )
        term = mm(hidden_ref[0], down)
        total = term if total is None else total + term

    @pl.when(step == 0)
    def _():
        acc[...] = total

    @pl.when(step > 0)
    def _():
        acc[...] += total

    @pl.when(step == steps - 1)
    def _():
        for g in range(segments):
            lines = [
                acc[(i * segments + g) * rows : (i * segments + g + 1) * rows, :][:, None, :]
                for i in range(2)
            ]
            out_ref[:, :, g * part : (g + 1) * part] = jnp.concatenate(lines, axis=1).astype(bf16)


def expert_outputs(hidden, low, high, out_rows):
    count, total_rows, depth = hidden.shape
    _, quarter, wide = low.shape
    part = wide // 2
    steps = count // 2
    rank = lax.axis_index("tensor").astype(jnp.int32).reshape(1)
    half_wide = total_rows // out_rows // 2 * part

    def block(k):
        return pl.BlockSpec(
            (1, total_rows, depth),
            lambda s, rank_ref: (lax.rem(rank_ref[0] + count - (2 * s + k), count), 0, 0),
        )

    pieces = pl.BlockSpec((2, quarter, wide), lambda s, rank_ref: (s, 0, 0))
    return pl.pallas_call(
        functools.partial(output_kernel, steps),
        grid_spec=pltpu.PrefetchScalarGridSpec(
            num_scalar_prefetch=1,
            grid=(steps,),
            in_specs=[block(0), block(1), pieces, pieces],
            out_specs=pl.BlockSpec((out_rows, 2, half_wide), lambda s, rank_ref: (0, 0, 0)),
            scratch_shapes=[pltpu.VMEM((total_rows, part), f32)],
        ),
        out_shape=jax.ShapeDtypeStruct((out_rows, 2, half_wide), bf16),
        compiler_params=pltpu.CompilerParams(vmem_limit_bytes=28 << 20),
        name="expert_outputs",
    )(rank, hidden, hidden, low, high)


def combine_kernel(stream_ref, routes_ref, values_ref, returned_ref, out_ref):
    part = stream_ref.shape[1]
    routes = routes_ref[...]
    values = values_ref[...].astype(f32)
    mix = (route_scale * values / jnp.sum(values, axis=0, keepdims=True)).astype(bf16).astype(f32)
    _, slot, expert_row = slots_of(routes, returned_ref.shape[0])
    weight = jnp.zeros(expert_row.shape, f32)
    for k in range(routes.shape[0]):
        weight = weight + jnp.where(routes[k : k + 1, :] == expert_row, mix[k : k + 1, :], 0.0)
    moe = stream_ref[...].astype(f32)
    segments = returned_ref.shape[2] // part
    for g in range(segments):
        pair = returned_ref[:, :, g * part : (g + 1) * part].astype(f32)
        for i in range(2):
            pick = jnp.where(slot == i * segments + g, weight, 0.0).astype(bf16)
            moe = moe + mm(pick, pair[:, i, :].astype(bf16), (0, 0))
    out_ref[...] = moe.astype(bf16)


def in_hbm(x):
    return pltpu.with_memory_space_constraint(x, pltpu.HBM)


def swap(x, axis):
    return lax.all_to_all(x, axis, split_axis=0, concat_axis=0, tiled=True)


def body(
    attn_out,
    out_weight,
    residual,
    norm_gain,
    gate_weights,
    up_weights,
    down_weights,
    routes,
    gate_values,
):
    tensor_count = lax.axis_size("tensor")
    dp_count = lax.axis_size("dp")
    expert_count = lax.axis_size("expert")
    own_tokens = attn_out.shape[0] // dp_count
    part = out_weight.shape[1] // tensor_count
    capacity = own_tokens * routes.shape[1] // expert_count

    parts = project(attn_out, out_weight, tensor_count, dp_count)
    parts = swap(parts.reshape(tensor_count * dp_count, own_tokens // 2, 2 * part), ("tensor", "dp"))
    stream, sent = pl.pallas_call(
        dispatch_kernel,
        out_shape=(
            jax.ShapeDtypeStruct((own_tokens, part), bf16),
            jax.ShapeDtypeStruct((expert_count, 2, capacity // 2 * part), bf16),
        ),
        compiler_params=pltpu.CompilerParams(vmem_limit_bytes=16 << 20),
        name="dispatch",
    )(parts, residual, routes.T)

    packed = pack_down(down_weights[0], tensor_count, dp_count)
    sent, *packed = lax.optimization_barrier((sent, *packed))
    received = swap(sent, "expert")
    rolled = [
        lax.ppermute(piece, "tensor", [(i, (i + s) % tensor_count) for i in range(tensor_count)])
        if s
        else piece
        for s, piece in enumerate(packed)
    ]
    received = received.reshape(expert_count, capacity * part)
    whole = lax.all_gather(received, "tensor", axis=0, tiled=False)
    hidden = hidden_units(
        in_hbm(whole),
        norm_gain,
        pltpu.with_memory_space_constraint(gate_weights[0], pltpu.VMEM),
        in_hbm(up_weights[0]),
    )
    hidden_all = lax.all_gather(hidden, "tensor", axis=0, tiled=False)
    mine = jnp.stack(rolled)
    theirs = lax.ppermute(mine, "dp", [(0, 1), (1, 0)])
    first = lax.axis_index("dp") == 0
    low = jnp.where(first, mine, theirs)
    high = jnp.where(first, theirs, mine)
    returned = swap(expert_outputs(in_hbm(hidden_all), low, high, expert_count), "expert")
    return pl.pallas_call(
        combine_kernel,
        out_shape=jax.ShapeDtypeStruct((own_tokens, part), bf16),
        compiler_params=pltpu.CompilerParams(vmem_limit_bytes=16 << 20),
        name="combine",
    )(stream, routes.T, gate_values.T, returned)


def solution(mesh):
    return jax.shard_map(
        body,
        mesh=mesh,
        in_specs=(
            P("expert", ("tensor", "dp")),
            P(("tensor", "dp"), None),
            P(("expert", "dp"), "tensor"),
            P(),
            P("expert", None, "tensor"),
            P("expert", None, "tensor"),
            P("expert", "tensor", None),
            P(("expert", "dp"), None),
            P(("expert", "dp"), None),
        ),
        out_specs=P(("expert", "dp"), "tensor"),
        check_vma=False,
    )
```

```python
import functools

import jax
import jax.numpy as jnp
from jax import lax
from jax.experimental import pallas as pl
from jax.experimental.pallas import tpu as pltpu
from jax.sharding import PartitionSpec as P


norm_eps = 1e-06
route_scale = 2.5
bf16 = jnp.bfloat16
f32 = jnp.float32


def mm(a, b, contract=(1, 0)):
    return lax.dot_general(
        a, b, (((contract[0],), (contract[1],)), ((), ())), preferred_element_type=f32
    )


def project_kernel(attn_ref, weight_ref, out_ref):
    own_half = out_ref.shape[2]
    part = out_ref.shape[3] // 2
    value = mm(attn_ref[...], weight_ref[...]).astype(bf16)
    for j in range(2):
        for d in range(out_ref.shape[1]):
            for h in range(2):
                row = (d * 2 + h) * own_half
                out_ref[j, d, :, h * part : (h + 1) * part] = value[
                    row : row + own_half, j * part : (j + 1) * part
                ]


def project(attn_out, out_weight, tensor_count, dp_count):
    rows, depth = attn_out.shape
    width = out_weight.shape[1]
    part = width // tensor_count
    own = rows // dp_count
    return pl.pallas_call(
        project_kernel,
        grid=(tensor_count // 2,),
        in_specs=[
            pl.BlockSpec((rows, depth), lambda s: (0, 0)),
            pl.BlockSpec((depth, 2 * part), lambda s: (0, s)),
        ],
        out_specs=pl.BlockSpec((2, dp_count, own // 2, 2 * part), lambda s: (s, 0, 0, 0)),
        out_shape=jax.ShapeDtypeStruct((tensor_count, dp_count, own // 2, 2 * part), bf16),
        compiler_params=pltpu.CompilerParams(vmem_limit_bytes=16 << 20),
        name="project",
    )(attn_out, in_hbm(out_weight))


def slots_of(routes, experts):
    own = routes.shape[1]
    expert_row = lax.broadcasted_iota(jnp.int32, (experts, own), 0)
    named = jnp.zeros((experts, own), f32)
    for k in range(routes.shape[0]):
        named = named + jnp.where(routes[k : k + 1, :] == expert_row, 1.0, 0.0)
    before = jnp.where(
        lax.broadcasted_iota(jnp.int32, (own, own), 0)
        < lax.broadcasted_iota(jnp.int32, (own, own), 1),
        1.0,
        0.0,
    ).astype(bf16)
    return named, mm(named.astype(bf16), before), expert_row


def dispatch_kernel(parts_ref, residual_ref, routes_ref, stream_ref, sent_ref):
    part = stream_ref.shape[1]
    total = parts_ref[0].astype(f32)
    for i in range(1, parts_ref.shape[0]):
        total = total + parts_ref[i].astype(f32)
    attn = jnp.concatenate([total[:, :part], total[:, part:]], axis=0)
    stream = (residual_ref[...].astype(f32) + attn).astype(bf16)
    stream_ref[...] = stream
    named, slot, _ = slots_of(routes_ref[...], sent_ref.shape[0])
    segments = sent_ref.shape[2] // part
    for g in range(segments):
        lines = []
        for i in range(2):
            pick = jnp.where(slot == i * segments + g, named, 0.0).astype(bf16)
            lines.append(mm(pick, stream)[:, None, :])
        sent_ref[:, :, g * part : (g + 1) * part] = jnp.concatenate(lines, axis=1).astype(bf16)


def pack_kernel(rank_ref, down_ref, *out_refs):
    count = len(out_refs)
    rows, wide = out_refs[0].shape
    part = wide // 2
    step = pl.program_id(0)
    for j in range(2):
        shift = lax.rem(2 * step + j + count - rank_ref[0], count)
        for s in range(count):

            @pl.when(shift == s)
            def _():
                for h in range(2):
                    out_refs[s][:, h * part : (h + 1) * part] = down_ref[
                        h * rows : (h + 1) * rows, j * part : (j + 1) * part
                    ]


def pack_down(down_weights, tensor_count, dp_count):
    rows, width = down_weights.shape[0] // dp_count, down_weights.shape[1]
    wide = 2 * (width // tensor_count)
    rank = jnp.stack([lax.axis_index("tensor"), lax.axis_index("dp")]).astype(jnp.int32)
    whole = pl.BlockSpec((rows // 2, wide), lambda s, rank_ref: (0, 0))
    return pl.pallas_call(
        pack_kernel,
        grid_spec=pltpu.PrefetchScalarGridSpec(
            num_scalar_prefetch=1,
            grid=(tensor_count // 2,),
            in_specs=[pl.BlockSpec((rows, wide), lambda s, rank_ref: (rank_ref[1], s))],
            out_specs=[whole] * tensor_count,
        ),
        out_shape=[jax.ShapeDtypeStruct((rows // 2, wide), bf16)] * tensor_count,
        compiler_params=pltpu.CompilerParams(vmem_limit_bytes=16 << 20),
        name="pack_down",
    )(rank, in_hbm(down_weights))


def hidden_kernel(steps, x_ref, gain_ref, gate_ref, up_ref, out_ref, gate_acc, up_acc, square_acc):
    step = pl.program_id(0)
    slices, _, part = gain_ref.shape
    rows = x_ref.shape[1]
    segments = x_ref.shape[2] // part
    width = part * slices * steps
    lanes = square_acc.shape[1]
    gate = up = None
    square = [None] * segments
    for k in range(slices):
        scaled = []
        for g in range(segments):
            wide = x_ref[k, :, g * part : (g + 1) * part].astype(f32)
            scaled.append((wide * gain_ref[k]).astype(bf16))
            powers = wide * wide
            for c in range(0, part, lanes):
                piece = powers[:, c : c + lanes]
                if piece.shape[1] < lanes:
                    piece = jnp.concatenate(
                        [piece, jnp.zeros((rows, lanes - piece.shape[1]), f32)], axis=1
                    )
                square[g] = piece if square[g] is None else square[g] + piece
        scaled = jnp.concatenate(scaled, axis=0)
        depth = slice(k * part, (k + 1) * part)
        whole_depth = pl.ds(pl.multiple_of((step * slices + k) * part, 64), part)
        gate_term = mm(scaled, gate_ref[whole_depth, :])
        up_term = mm(scaled, up_ref[depth, :])
        gate = gate_term if gate is None else gate + gate_term
        up = up_term if up is None else up + up_term
    square = jnp.concatenate(square, axis=0)

    @pl.when(step == 0)
    def _():
        gate_acc[...] = gate
        up_acc[...] = up
        square_acc[...] = square

    @pl.when(step > 0)
    def _():
        gate_acc[...] += gate
        up_acc[...] += up
        square_acc[...] += square

    @pl.when(step == steps - 1)
    def _():
        mean = jnp.sum(square_acc[...], axis=1, keepdims=True) / width
        inverse = lax.rsqrt(mean + norm_eps)
        gate = inverse * gate_acc[...]
        up = inverse * up_acc[...]
        out_ref[...] = (jax.nn.silu(gate) * up).astype(bf16)


def hidden_units(x, gain, gate_weights, up_weights):
    count, rows, wide = x.shape
    width, hidden_width = gate_weights.shape
    part = width // count
    total_rows = rows * (wide // part)
    slices = 2
    steps = count // slices
    return pl.pallas_call(
        functools.partial(hidden_kernel, steps),
        grid=(steps,),
        in_specs=[
            pl.BlockSpec((slices, rows, wide), lambda s: (s, 0, 0)),
            pl.BlockSpec((slices, 1, part), lambda s: (s, 0, 0)),
            pl.BlockSpec(memory_space=pltpu.VMEM),
            pl.BlockSpec((slices * part, hidden_width), lambda s: (s, 0)),
        ],
        out_specs=pl.BlockSpec((total_rows, hidden_width), lambda s: (0, 0)),
        out_shape=pltpu.HBM((total_rows, hidden_width), bf16),
        scratch_shapes=[
            pltpu.VMEM((total_rows, hidden_width), f32),
            pltpu.VMEM((total_rows, hidden_width), f32),
            pltpu.VMEM((total_rows, 128), f32),
        ],
        compiler_params=pltpu.CompilerParams(vmem_limit_bytes=28 << 20),
        name="hidden_units",
    )(x, gain.reshape(count, 1, part), gate_weights, up_weights)


def output_kernel(steps, rank_ref, first_ref, second_ref, low_ref, high_ref, out_ref, acc):
    step = pl.program_id(0)
    rows = out_ref.shape[0]
    part = acc.shape[1]
    segments = out_ref.shape[2] // part
    total = None
    for k, hidden_ref in enumerate((first_ref, second_ref)):
        down = jnp.concatenate(
            [
                ref[k, :, h * part : (h + 1) * part]
                for ref in (low_ref, high_ref)
                for h in range(2)
            ],
            axis=0,
        )
        term = mm(hidden_ref[0], down)
        total = term if total is None else total + term

    @pl.when(step == 0)
    def _():
        acc[...] = total

    @pl.when(step > 0)
    def _():
        acc[...] += total

    @pl.when(step == steps - 1)
    def _():
        for g in range(segments):
            lines = [
                acc[(i * segments + g) * rows : (i * segments + g + 1) * rows, :][:, None, :]
                for i in range(2)
            ]
            out_ref[:, :, g * part : (g + 1) * part] = jnp.concatenate(lines, axis=1).astype(bf16)


def expert_outputs(hidden, low, high, out_rows):
    count, total_rows, depth = hidden.shape
    _, quarter, wide = low.shape
    part = wide // 2
    steps = count // 2
    rank = lax.axis_index("tensor").astype(jnp.int32).reshape(1)
    half_wide = total_rows // out_rows // 2 * part

    def block(k):
        return pl.BlockSpec(
            (1, total_rows, depth),
            lambda s, rank_ref: (lax.rem(rank_ref[0] + count - (2 * s + k), count), 0, 0),
        )

    pieces = pl.BlockSpec((2, quarter, wide), lambda s, rank_ref: (s, 0, 0))
    return pl.pallas_call(
        functools.partial(output_kernel, steps),
        grid_spec=pltpu.PrefetchScalarGridSpec(
            num_scalar_prefetch=1,
            grid=(steps,),
            in_specs=[block(0), block(1), pieces, pieces],
            out_specs=pl.BlockSpec((out_rows, 2, half_wide), lambda s, rank_ref: (0, 0, 0)),
            scratch_shapes=[pltpu.VMEM((total_rows, part), f32)],
        ),
        out_shape=jax.ShapeDtypeStruct((out_rows, 2, half_wide), bf16),
        compiler_params=pltpu.CompilerParams(vmem_limit_bytes=28 << 20),
        name="expert_outputs",
    )(rank, hidden, hidden, low, high)


def combine_kernel(stream_ref, routes_ref, values_ref, returned_ref, out_ref):
    part = stream_ref.shape[1]
    routes = routes_ref[...]
    values = values_ref[...].astype(f32)
    mix = (route_scale * values / jnp.sum(values, axis=0, keepdims=True)).astype(bf16).astype(f32)
    _, slot, expert_row = slots_of(routes, returned_ref.shape[0])
    weight = jnp.zeros(expert_row.shape, f32)
    for k in range(routes.shape[0]):
        weight = weight + jnp.where(routes[k : k + 1, :] == expert_row, mix[k : k + 1, :], 0.0)
    moe = stream_ref[...].astype(f32)
    segments = returned_ref.shape[2] // part
    for g in range(segments):
        pair = returned_ref[:, :, g * part : (g + 1) * part].astype(f32)
        for i in range(2):
            pick = jnp.where(slot == i * segments + g, weight, 0.0).astype(bf16)
            moe = moe + mm(pick, pair[:, i, :].astype(bf16), (0, 0))
    out_ref[...] = moe.astype(bf16)


def in_hbm(x):
    return pltpu.with_memory_space_constraint(x, pltpu.HBM)


def swap(x, axis):
    return lax.all_to_all(x, axis, split_axis=0, concat_axis=0, tiled=True)


def body(
    attn_out,
    out_weight,
    residual,
    norm_gain,
    gate_weights,
    up_weights,
    down_weights,
    routes,
    gate_values,
):
    tensor_count = lax.axis_size("tensor")
    dp_count = lax.axis_size("dp")
    expert_count = lax.axis_size("expert")
    own_tokens = attn_out.shape[0] // dp_count
    part = out_weight.shape[1] // tensor_count
    capacity = own_tokens * routes.shape[1] // expert_count

    parts = project(attn_out, out_weight, tensor_count, dp_count)
    parts = swap(
        parts.reshape(tensor_count * dp_count, own_tokens // 2, 2 * part), ("tensor", "dp")
    )
    rolled = list(pack_down(down_weights[0], tensor_count, dp_count))
    far = range(2, tensor_count - 2)
    near = [s for s in range(1, tensor_count) if s not in far]

    def roll(s):
        moves = [(i, (i + s) % tensor_count) for i in range(tensor_count)]
        return lax.ppermute(rolled[s], "tensor", moves)

    for s in far:
        rolled[s] = roll(s)
    stream, sent = pl.pallas_call(
        dispatch_kernel,
        out_shape=(
            jax.ShapeDtypeStruct((own_tokens, part), bf16),
            jax.ShapeDtypeStruct((expert_count, 2, capacity // 2 * part), bf16),
        ),
        compiler_params=pltpu.CompilerParams(vmem_limit_bytes=16 << 20),
        name="dispatch",
    )(parts, residual, routes.T)

    sent, *held = lax.optimization_barrier((sent, *[rolled[s] for s in near]))
    for s, piece in zip(near, held):
        rolled[s] = piece
    received = swap(sent, "expert")
    for s in near:
        rolled[s] = roll(s)
    received = received.reshape(expert_count, capacity * part)
    whole = lax.all_gather(received, "tensor", axis=0, tiled=False)
    hidden = hidden_units(
        in_hbm(whole),
        norm_gain,
        pltpu.with_memory_space_constraint(gate_weights[0], pltpu.VMEM),
        in_hbm(up_weights[0]),
    )
    hidden_all = lax.all_gather(hidden, "tensor", axis=0, tiled=False)
    mine = jnp.stack(rolled)
    theirs = lax.ppermute(mine, "dp", [(0, 1), (1, 0)])
    first = lax.axis_index("dp") == 0
    low = jnp.where(first, mine, theirs)
    high = jnp.where(first, theirs, mine)
    returned = swap(expert_outputs(in_hbm(hidden_all), low, high, expert_count), "expert")
    return pl.pallas_call(
        combine_kernel,
        out_shape=jax.ShapeDtypeStruct((own_tokens, part), bf16),
        compiler_params=pltpu.CompilerParams(vmem_limit_bytes=16 << 20),
        name="combine",
    )(stream, routes.T, gate_values.T, returned)


def solution(mesh):
    return jax.shard_map(
        body,
        mesh=mesh,
        in_specs=(
            P("expert", ("tensor", "dp")),
            P(("tensor", "dp"), None),
            P(("expert", "dp"), "tensor"),
            P(),
            P("expert", None, "tensor"),
            P("expert", None, "tensor"),
            P("expert", "tensor", None),
            P(("expert", "dp"), None),
            P(("expert", "dp"), None),
        ),
        out_specs=P(("expert", "dp"), "tensor"),
        check_vma=False,
    )
```
